32 devices in a mesh: user: 8 (over y, x, core), item: 4 (over z).
Axes of the slice: x: 2, y: 2, z: 4, core: 2. Of those that a mesh axis runs over, the one named last changes fastest.
Arguments:
- user_comps: bfloat16 [1024, 512], P(('user', 'item')), may hold values from -6 to 6
- item_text: bfloat16 [1024, 1024], P(('user', 'item')), may hold values from -6 to 6
- item_proj: bfloat16 [1024, 512], replicated, may hold values from -0.1875 to 0.1875
- w_in: float32 [64, 128], replicated, may hold values from -0.75 to 0.75
- b_in: float32 [128], replicated, may hold values from -4 to 4
- w_out: float32 [128, 64], replicated, may hold values from -1.5 to 1.5
- b_out: float32 [64], replicated, may hold values from -4 to 4
- pair_user: int32 [32768], P(('user', 'item')), may hold values from 0 to 127
- pair_item: int32 [32768], P(('user', 'item')), may hold values from 0 to 255
- teacher: float32 [32768], P(('user', 'item')), may hold values from -12 to 12
Outputs:
- user_grad: float32 [1024, 512], P(('user', 'item'))
- item_grad: float32 [1024, 512], P(('user', 'item'))
The draws below stay inside these ranges and needn't reach their ends.
Inputs may be any that keep to these rules, and one draw needn't show every extreme that they name: `pair_user`: index of a user among the 128 users of the pair's tile. `pair_item`: index of an item among the 256 items of the pair's tile.
All inputs are finite; a program needn't handle non-finite values.
Results may differ from the reference program's by a relative error of at most 0.0058.
Values may be sent and summed in bfloat16 or wider, within the bound.
No kernel may reach another device: no remote copies, remote signals or barrier semaphores. Data moves between devices by JAX's collectives and lax.ppermute only.
A program may use at most 64 MiB of HBM per device.

```python
import math
import jax
import jax.numpy as jnp
from jax import lax

DT = 1024
COMPS = 8
CDIM = 64
GATE_HIDDEN = 128
USER_DEV = 128
ITEM_DEV = 256
PAIR_DEV = 1024
GATES = 64
USERS = 1024
ITEMS = 1024
ISUB = 32
PAIRS = 32768
N_USER = 8
N_ITEM = 4


def place_ends(drawn, rng, smallest, top_value):
    dims = drawn.shape
    spot = [jax.random.randint(jax.random.fold_in(rng, axis), (), 0, dims[axis]) for axis in range(len(dims))]
    drawn = drawn.at[tuple(spot)].set(smallest)
    longest = dims.index(max(dims))
    spot[longest] = (spot[longest] + 1) % dims[longest]
    return drawn.at[tuple(spot)].set(top_value)


def block_scale(key, extent, shards, least, top_value):
    def one(axis_at, parts):
        heights = jax.random.uniform(jax.random.fold_in(jax.random.fold_in(key, 6), axis_at), (parts,), jnp.float32, least / len(shards), top_value / len(shards))
        return jnp.repeat(jnp.exp(heights), extent[axis_at] // parts).reshape((-1,) + (1,) * (len(extent) - axis_at - 1))

    loudness = one(*shards[0])
    for cut in shards[1:]:
        loudness = loudness * one(*cut)
    return loudness


def noise(key, shape, deviation, bound, split=(), kind=jnp.bfloat16):
    drawn = deviation * jax.random.normal(key, shape, jnp.float32)
    if split:
        drawn = drawn * block_scale(key, shape, split, -0.22, 0.18)
    return jnp.clip(drawn, -bound, bound).astype(kind)


def setup_inputs(seed: int = 0) -> dict:
    splits = jax.random.split(jax.random.key(seed), 11)
    return {
        "user_comps": noise(splits[0], (USERS, COMPS * CDIM), 1.0, 6.0, ((0, 32),)),
        "item_text": noise(splits[1], (ITEMS, DT), 1.0, 6.0, ((0, 32),)),
        "item_proj": noise(splits[2], (DT, COMPS * CDIM), DT ** -0.5, 0.1875),
        "w_in": noise(splits[3], (GATES, GATE_HIDDEN), GATES ** -0.5, 0.75, (), jnp.float32),
        "b_in": noise(splits[4], (GATE_HIDDEN,), 1.0, 4.0, (), jnp.float32),
        "w_out": noise(splits[5], (GATE_HIDDEN, GATES), 16 ** -0.5, 1.5, (), jnp.float32),
        "b_out": noise(splits[6], (GATES,), 1.0, 4.0, (), jnp.float32),
        "pair_user": place_ends(jax.random.randint(splits[7], (PAIRS,), 0, USER_DEV), jax.random.fold_in(splits[7], 1), 0, USER_DEV - 1).astype(jnp.int32),
        "pair_item": place_ends(jax.random.randint(splits[8], (PAIRS,), 0, ITEM_DEV), jax.random.fold_in(splits[8], 1), 0, ITEM_DEV - 1).astype(jnp.int32),
        "teacher": noise(splits[9], (PAIRS,), 2.0, 12.0, ((0, 32),), jnp.float32),
    }


gate_cap = 8.0

def component_norm(values):
    mean_square = lax.optimization_barrier(jnp.mean(values * values, axis=-1, keepdims=True))
    return values * lax.rsqrt(mean_square + 1e-06)

def pair_grads(user_portion, item_portion, target, w_in, b_in, w_out, b_out, loss_scale):
    width = user_portion.shape[-1]
    reciprocal_norm = 1.0 / math.sqrt(width)
    user_broadcast = user_portion.astype(jnp.float32)
    item_broadcast = item_portion.astype(jnp.float32)
    mixture_logits = jnp.einsum('xvw,xzw->xvz', user_broadcast, item_broadcast, precision=lax.Precision.HIGHEST) * reciprocal_norm
    pair_count = mixture_logits.shape[0]
    flat_logits = mixture_logits.reshape(pair_count, -1)
    hidden_in = jnp.dot(flat_logits, w_in, precision=lax.Precision.HIGHEST) + b_in
    sig_pre = jax.nn.sigmoid(hidden_in)
    hidden = hidden_in * sig_pre
    gate_raw = jnp.dot(hidden, w_out, precision=lax.Precision.HIGHEST) + b_out
    capped = jnp.tanh(gate_raw / gate_cap)
    exp_gate = jnp.exp(gate_cap * capped)
    weights = exp_gate / lax.optimization_barrier(jnp.sum(exp_gate, axis=-1, keepdims=True))
    student = lax.optimization_barrier(jnp.sum(weights * flat_logits, axis=-1))
    residual_w = (student - target) * loss_scale
    d_gate = weights * (flat_logits - student[:, None]) * (1.0 - capped * capped)
    d_hidden = jnp.dot(d_gate, w_out.T, precision=lax.Precision.HIGHEST)
    d_pre = d_hidden * sig_pre * (1.0 + hidden_in * (1.0 - sig_pre))
    d_flat = residual_w[:, None] * (weights + jnp.dot(d_pre, w_in.T, precision=lax.Precision.HIGHEST))
    logit_gradient = (d_flat * reciprocal_norm).astype(jnp.bfloat16).reshape(mixture_logits.shape).astype(jnp.float32)
    user_gradient = jnp.einsum('ftz,fzr->ftr', logit_gradient, item_broadcast, precision=lax.Precision.HIGHEST)
    item_gradient = jnp.einsum('uwx,uwz->uxz', logit_gradient, user_broadcast, precision=lax.Precision.HIGHEST)
    return (user_gradient, item_gradient)

def reference(user_comps, item_text, item_proj, w_in, b_in, w_out, b_out, pair_user, pair_item, teacher):
    user_three = user_comps.reshape(USERS, COMPS, CDIM)
    mixed = jnp.dot(item_text, item_proj, preferred_element_type=jnp.float32).reshape(ITEMS, COMPS, CDIM)
    item_three = component_norm(mixed).astype(jnp.bfloat16)
    loss_scale = 2.0 * math.sqrt(USER_DEV / (PAIR_DEV * N_ITEM))
    tile_total = N_USER * N_ITEM
    user_ids = pair_user.reshape(tile_total, PAIR_DEV)
    item_ids = pair_item.reshape(tile_total, PAIR_DEV)
    targets = teacher.reshape(tile_total, PAIR_DEV)
    tile_ids = jnp.arange(tile_total, dtype=jnp.int32)

    def one_tile(sums, inputs):
        tile_id, local_user, local_item, target = inputs
        row_index = tile_id // N_ITEM
        col_index = tile_id % N_ITEM
        global_user = (row_index * USER_DEV + local_user).astype(jnp.int32)
        global_item = ((local_item // ISUB * N_ITEM + col_index) * ISUB + local_item % ISUB).astype(jnp.int32)
        user_gradient, item_gradient = pair_grads(user_three[global_user], item_three[global_item], target, w_in, b_in, w_out, b_out, loss_scale)
        return ((sums[0].at[global_user].add(user_gradient), sums[1].at[global_item].add(item_gradient)), None)
    start_sums = (jnp.zeros((USERS, COMPS, CDIM), jnp.float32), jnp.zeros((ITEMS, COMPS, CDIM), jnp.float32))
    (grad_users, grad_items), _ = lax.scan(one_tile, start_sums, (tile_ids, user_ids, item_ids, targets))
    return (grad_users.reshape(USERS, COMPS * CDIM), grad_items.reshape(ITEMS, COMPS * CDIM))
```

```python
import functools
import math

import jax
import jax.numpy as jnp
from jax import lax
from jax.experimental import pallas as pl
from jax.experimental.pallas import tpu as pltpu
from jax.sharding import PartitionSpec as P

COMPS = 8
CDIM = 64
gate_cap = 8.0
F32 = jnp.float32
BF16 = jnp.bfloat16
VMEM = pl.BlockSpec(memory_space=pltpu.VMEM)


def bits_of(size):
    return size.bit_length() - 1


def exchange(value, axis, step):
    size = lax.axis_size(axis)
    return lax.ppermute(value, axis, [(i, i ^ step) for i in range(size)])


def round_steps(size):
    steps = [1 << bit for bit in range(1, bits_of(size))]
    return steps + ([1] if size > 1 else [])


def place_of(block, me, size):
    apart = block ^ me
    if size < 4:
        return apart
    return (apart >> 1) | ((apart & 1) << (bits_of(size) - 1))


def gather_rows(value, axis):
    for step in round_steps(lax.axis_size(axis)):
        value = jnp.concatenate([value, exchange(value, axis, step)], axis=0)
    return value


def scatter_rows(keep, send, axis):
    steps = round_steps(lax.axis_size(axis))[::-1]
    for at, step in enumerate(steps):
        total = keep + exchange(send, axis, step).astype(F32)
        if at + 1 < len(steps):
            half = total.shape[0] // 2
            keep, send = total[:half], total[half:].astype(BF16)
    return total


def project_kernel(text_ref, proj_ref, out_ref):
    mixed = jnp.dot(text_ref[...], proj_ref[...], preferred_element_type=F32)
    parts = []
    for at in range(COMPS):
        part = mixed[:, at * CDIM : (at + 1) * CDIM]
        square = jnp.mean(part * part, axis=-1, keepdims=True)
        parts.append(part * lax.rsqrt(square + 1e-06))
    out_ref[...] = jnp.concatenate(parts, axis=1).astype(BF16)


def project_rows(text, proj):
    return pl.pallas_call(
        project_kernel,
        out_shape=jax.ShapeDtypeStruct((text.shape[0], proj.shape[1]), BF16),
        in_specs=[VMEM, VMEM],
        out_specs=VMEM,
        compiler_params=pltpu.CompilerParams(vmem_limit_bytes=8 << 20),
        name="project",
    )(text, proj)


def halves(value):
    upper = value.astype(BF16)
    return upper, (value - upper.astype(F32)).astype(BF16)


def weight_stack(weight, axis):
    upper, lower = halves(weight)
    return jnp.concatenate([upper, lower, upper], axis=axis)


def value_stack(value, bias):
    upper, lower = halves(value)
    pieces = [upper, upper, lower]
    if bias:
        pieces.append(jnp.ones((16, value.shape[1]), BF16))
    return jnp.concatenate(pieces, axis=0)


def bias_rows(bias):
    upper, rest = bias.astype(BF16), bias
    rows = [upper]
    for _ in range(2):
        rest = rest - upper.astype(F32)
        upper = rest.astype(BF16)
        rows.append(upper)
    rows.append(jnp.zeros((13, bias.shape[1]), BF16))
    return jnp.concatenate([r.astype(F32) for r in rows], axis=0).astype(BF16)


def fold_rows(parts):
    place = lax.broadcasted_iota(jnp.int32, parts[0].shape, 0)
    width = 4
    while len(parts) > 1:
        low = (place & width) == 0
        half = len(parts) // 2
        merged = []
        for at in range(half):
            one, two = parts[at], parts[at + half]
            stay = jnp.where(low, one, two)
            move = jnp.where(low, two, one)
            merged.append(stay + pltpu.roll(move, width, 0) if width == 4 else stay + shift_rows(move, width, low))
        parts = merged
        width //= 2
    return parts[0]


def shift_rows(value, width, low):
    return jnp.where(low, pltpu.roll(value, 8 - width, 0), pltpu.roll(value, width, 0))


def pair_kernel(
    sizes,
    loss_scale,
    users_ref,
    items_ref,
    w_in_ref,
    b_in_ref,
    w_out_ref,
    b_out_ref,
    pair_user_ref,
    pair_item_ref,
    teacher_ref,
    user_keep_ref,
    user_send_ref,
    item_keep_ref,
    item_send_ref,
    user_hot,
    item_hot,
    user_pairs,
    item_pairs,
    logits_ref,
    grad_ref,
    user_terms,
    item_terms,
):
    n_user, n_item = sizes
    user_rows, item_rows = users_ref.shape[0], items_ref.shape[0]
    pairs = pair_user_ref.shape[1]
    me_user, me_item = lax.axis_index("user"), lax.axis_index("item")
    gates = COMPS * COMPS
    wide = 256
    tile = 128
    scale = 1.0 / math.sqrt(CDIM)

    def spots(index, rows, size, me):
        each = rows // size
        return place_of(index // each, me, size) * each + index % each

    users_t = users_ref[...].T
    items_t = items_ref[...].T
    w_in, w_out = w_in_ref[...], w_out_ref[...]
    w_in_fwd = jnp.concatenate([weight_stack(w_in, 0), bias_rows(b_in_ref[...])], axis=0).T
    w_out_fwd = jnp.concatenate([weight_stack(w_out, 0), bias_rows(b_out_ref[...])], axis=0).T
    w_in_bwd = weight_stack(w_in, 1)
    w_out_bwd = weight_stack(w_out, 1)

    def dot(one, two):
        return jnp.dot(one, two, preferred_element_type=F32)

    for block in range(pairs // wide):
        lanes = slice(block * wide, (block + 1) * wide)
        user_at = spots(pair_user_ref[:, lanes], user_rows, n_item, me_item)
        item_at = spots(pair_item_ref[:, lanes], item_rows, n_user, me_user)
        hot = lax.broadcasted_iota(jnp.int32, (user_rows, wide), 0) == user_at
        user_hot[:, lanes] = jnp.where(hot, 1.0, 0.0).astype(BF16)
        hot = lax.broadcasted_iota(jnp.int32, (item_rows, wide), 0) == item_at
        item_hot[:, lanes] = jnp.where(hot, 1.0, 0.0).astype(BF16)
        user_pairs[:, lanes] = dot(users_t, user_hot[:, lanes])
        item_pairs[:, lanes] = dot(items_t, item_hot[:, lanes])

        for sub in range(wide // tile):
            span = slice(block * wide + sub * tile, block * wide + (sub + 1) * tile)
            for c in range(COMPS):
                parts = []
                for k in range(COMPS):
                    total = None
                    for j in range(CDIM // 8):
                        u = user_pairs[c * CDIM + j * 8 : c * CDIM + (j + 1) * 8, span]
                        v = item_pairs[k * CDIM + j * 8 : k * CDIM + (j + 1) * 8, span]
                        total = u * v if total is None else total + u * v
                    parts.append(total)
                logits_ref[c * COMPS : (c + 1) * COMPS, span] = fold_rows(parts) * scale

        logits = logits_ref[:, lanes]
        pre = dot(w_in_fwd, value_stack(logits, True))
        sig = jax.nn.sigmoid(pre)
        hidden = pre * sig
        raw = dot(w_out_fwd, value_stack(hidden, True))
        capped = jnp.tanh(raw * (1.0 / gate_cap))
        powers = jnp.exp(gate_cap * capped)
        weights = powers * (1.0 / jnp.sum(powers, axis=0, keepdims=True))
        student = jnp.sum(weights * logits, axis=0, keepdims=True)
        residual = (student - teacher_ref[:, lanes]) * loss_scale
        d_gate = weights * (logits - student) * (1.0 - capped * capped)
        d_hidden = dot(w_out_bwd, value_stack(d_gate, False))
        d_pre = d_hidden * sig * (1.0 + pre * (1.0 - sig))
        d_flat = residual * (weights + dot(w_in_bwd, value_stack(d_pre, False)))
        grad_ref[:, lanes] = (d_flat * scale).astype(BF16).astype(F32)

        for sub in range(wide // tile):
            span = slice(block * wide + sub * tile, block * wide + (sub + 1) * tile)
            for terms, pairs_ref, row in (
                (user_terms, item_pairs, lambda c, k: c * COMPS + k),
                (item_terms, user_pairs, lambda k, c: c * COMPS + k),
            ):
                for one in range(COMPS):
                    spread = [
                        jnp.broadcast_to(grad_ref[row(one, two) : row(one, two) + 1, span], (16, tile))
                        for two in range(COMPS)
                    ]
                    for j in range(CDIM // 16):
                        total = None
                        for two in range(COMPS):
                            at = two * CDIM + j * 16
                            term = spread[two] * pairs_ref[at : at + 16, span]
                            total = term if total is None else total + term
                        at = one * CDIM + j * 16
                        terms[at : at + 16, span] = total.astype(BF16)

    def collect(hot, terms, keep_ref, send_ref):
        total = lax.dot_general(
            hot[...], terms[...], (((1,), (1,)), ((), ())), preferred_element_type=F32
        )
        half = total.shape[0] // 2
        keep_ref[...] = total[:half]
        send_ref[...] = total[half:].astype(BF16)

    collect(user_hot, user_terms, user_keep_ref, user_send_ref)
    collect(item_hot, item_terms, item_keep_ref, item_send_ref)


def pair_terms(users, items, w_in, b_in, w_out, b_out, pair_user, pair_item, teacher, sizes, loss_scale):
    pairs = pair_user.shape[0]
    user_rows, item_rows = users.shape[0], items.shape[0]
    width = COMPS * CDIM

    def out(rows):
        return [
            jax.ShapeDtypeStruct((rows // 2, width), F32),
            jax.ShapeDtypeStruct((rows // 2, width), BF16),
        ]

    return pl.pallas_call(
        functools.partial(pair_kernel, sizes, loss_scale),
        out_shape=out(user_rows) + out(item_rows),
        in_specs=[VMEM] * 9,
        out_specs=[VMEM] * 4,
        scratch_shapes=[
            pltpu.VMEM((user_rows, pairs), BF16),
            pltpu.VMEM((item_rows, pairs), BF16),
            pltpu.VMEM((width, pairs), F32),
            pltpu.VMEM((width, pairs), F32),
            pltpu.VMEM((COMPS * COMPS, pairs), F32),
            pltpu.VMEM((COMPS * COMPS, pairs), F32),
            pltpu.VMEM((width, pairs), BF16),
            pltpu.VMEM((width, pairs), BF16),
        ],
        compiler_params=pltpu.CompilerParams(vmem_limit_bytes=24 << 20),
        name="pairs",
    )(
        users,
        items,
        w_in,
        b_in.reshape(1, -1),
        w_out,
        b_out.reshape(1, -1),
        pair_user.reshape(1, -1),
        pair_item.reshape(1, -1),
        teacher.reshape(1, -1),
    )


def local(user_comps, item_text, item_proj, w_in, b_in, w_out, b_out, pair_user, pair_item, teacher):
    n_user, n_item = lax.axis_size("user"), lax.axis_size("item")
    users = gather_rows(user_comps, "item")
    items = gather_rows(project_rows(item_text, item_proj), "user")
    loss_scale = 2.0 * math.sqrt(users.shape[0] / (pair_user.shape[0] * n_item))
    user_keep, user_send, item_keep, item_send = pair_terms(
        users, items, w_in, b_in, w_out, b_out, pair_user, pair_item, teacher, (n_user, n_item), loss_scale
    )
    return scatter_rows(user_keep, user_send, "item"), scatter_rows(item_keep, item_send, "user")


def solution(mesh):
    split = P(("user", "item"))
    rows = P(("user", "item"), None)
    in_specs = (rows, rows, P(), P(), P(), P(), P(), split, split, split)
    return jax.shard_map(local, mesh=mesh, in_specs=in_specs, out_specs=(rows, rows), check_vma=False)
```

```python
import functools
import math

import jax
import jax.numpy as jnp
from jax import lax
from jax.experimental import pallas as pl
from jax.experimental.pallas import tpu as pltpu
from jax.sharding import PartitionSpec as P


COMPS = 8
CDIM = 64
gate_cap = 8.0
F32 = jnp.float32
BF16 = jnp.bfloat16
VMEM = pl.BlockSpec(memory_space=pltpu.VMEM)
WIDE = 256
TILE = 128


def bits_of(size):
    return size.bit_length() - 1


def exchange(value, axis, step):
    size = lax.axis_size(axis)
    return lax.ppermute(value, axis, [(i, i ^ step) for i in range(size)])


def round_steps(size):
    steps = [1 << bit for bit in range(1, bits_of(size))]
    return steps + ([1] if size > 1 else [])


def place_of(block, me, size):
    apart = block ^ me
    if size < 4:
        return apart
    return (apart >> 1) | ((apart & 1) << (bits_of(size) - 1))


def ready_kernel(out_ref):
    out_ref[...] = jnp.zeros_like(out_ref)


def project_kernel(text_ref, proj_ref, ready_ref, out_ref):
    mixed = jnp.dot(text_ref[...], proj_ref[...], preferred_element_type=F32)
    parts = []
    for at in range(COMPS):
        part = mixed[:, at * CDIM : (at + 1) * CDIM]
        square = jnp.mean(part * part, axis=-1, keepdims=True)
        parts.append(part * lax.rsqrt(square + 1e-06))
    out_ref[...] = jnp.concatenate(parts, axis=1).astype(BF16)


def halves(value):
    upper = value.astype(BF16)
    return upper, (value - upper.astype(F32)).astype(BF16)


def weight_stack(weight, axis):
    upper, lower = halves(weight)
    return jnp.concatenate([upper, lower, upper], axis=axis)


def value_stack(value, bias):
    upper, lower = halves(value)
    pieces = [upper, upper, lower]
    if bias:
        pieces.append(jnp.ones((16, value.shape[1]), BF16))
    return jnp.concatenate(pieces, axis=0)


def bias_rows(bias):
    upper, rest = bias.astype(BF16), bias
    rows = [upper]
    for _ in range(2):
        rest = rest - upper.astype(F32)
        upper = rest.astype(BF16)
        rows.append(upper)
    rows.append(jnp.zeros((13, bias.shape[1]), BF16))
    return jnp.concatenate([r.astype(F32) for r in rows], axis=0).astype(BF16)


def fold_rows(parts):
    place = lax.broadcasted_iota(jnp.int32, parts[0].shape, 0)
    width = 4
    while len(parts) > 1:
        low = (place & width) == 0
        half = len(parts) // 2
        merged = []
        for at in range(half):
            one, two = parts[at], parts[at + half]
            stay = jnp.where(low, one, two)
            move = jnp.where(low, two, one)
            merged.append(stay + pltpu.roll(move, width, 0) if width == 4 else stay + shift_rows(move, width, low))
        parts = merged
        width //= 2
    return parts[0]


def shift_rows(value, width, low):
    return jnp.where(low, pltpu.roll(value, 8 - width, 0), pltpu.roll(value, width, 0))


def dot(one, two):
    return jnp.dot(one, two, preferred_element_type=F32)


def hot_rows(index, rows, size, me):
    each = rows // size
    spot = place_of(index // each, me, size) * each + index % each
    hot = lax.broadcasted_iota(jnp.int32, (rows, index.shape[1]), 0) == spot
    return jnp.where(hot, 1.0, 0.0).astype(BF16)


def user_kernel(
    sizes,
    users_ref,
    w_in_ref,
    b_in_ref,
    w_out_ref,
    b_out_ref,
    pair_user_ref,
    pair_item_ref,
    teacher_ref,
    user_pairs,
    user_hot,
    item_hot,
    w_in_fwd,
    w_out_fwd,
    w_in_bwd,
    w_out_bwd,
    target,
):
    n_user, n_item = sizes
    user_rows, item_rows = user_hot.shape[0], item_hot.shape[0]
    me_user, me_item = lax.axis_index("user"), lax.axis_index("item")
    w_in, w_out = w_in_ref[...], w_out_ref[...]
    w_in_fwd[...] = jnp.concatenate([weight_stack(w_in, 0), bias_rows(b_in_ref[...])], axis=0).T
    w_out_fwd[...] = jnp.concatenate([weight_stack(w_out, 0), bias_rows(b_out_ref[...])], axis=0).T
    w_in_bwd[...] = weight_stack(w_in, 1)
    w_out_bwd[...] = weight_stack(w_out, 1)
    target[...] = teacher_ref[...]
    users_t = users_ref[...].T
    for block in range(user_hot.shape[1] // WIDE):
        lanes = slice(block * WIDE, (block + 1) * WIDE)
        hot = hot_rows(pair_user_ref[:, lanes], user_rows, n_item, me_item)
        user_hot[:, lanes] = hot
        user_pairs[:, lanes] = dot(users_t, hot)
        item_hot[:, lanes] = hot_rows(pair_item_ref[:, lanes], item_rows, n_user, me_user)


def pair_gradients(grad_ref, pairs_ref, terms, span, row):
    for one in range(COMPS):
        spread = [
            jnp.broadcast_to(grad_ref[row(one, two) : row(one, two) + 1, span], (16, TILE)) for two in range(COMPS)
        ]
        for j in range(CDIM // 16):
            total = None
            for two in range(COMPS):
                at = two * CDIM + j * 16
                term = spread[two] * pairs_ref[at : at + 16, span]
                total = term if total is None else total + term
            at = one * CDIM + j * 16
            terms[at : at + 16, span] = total.astype(BF16)


def collect(hot, terms, keep_ref, send_ref):
    total = lax.dot_general(hot[...], terms[...], (((1,), (1,)), ((), ())), preferred_element_type=F32)
    half = total.shape[0] // 2
    keep_ref[...] = total[:half]
    send_ref[...] = total[half:].astype(BF16)


def pair_kernel(
    loss_scale,
    items_ref,
    user_pairs,
    user_hot,
    item_hot,
    w_in_fwd,
    w_out_fwd,
    w_in_bwd,
    w_out_bwd,
    target,
    user_keep_ref,
    user_send_ref,
    grad_ref,
    item_pairs,
    logits_ref,
    user_terms,
):
    pairs = user_hot.shape[1]
    blocks = pairs // WIDE
    scale = 1.0 / math.sqrt(CDIM)
    items_t = items_ref[...].T

    def gather(block):
        lanes = slice(block * WIDE, (block + 1) * WIDE)
        item_pairs[:, lanes] = dot(items_t, item_hot[:, lanes])

    def spans(block):
        return [slice(block * WIDE + at, block * WIDE + at + TILE) for at in range(0, WIDE, TILE)]

    def make_logits(block):
        for span in spans(block):
            for c in range(COMPS):
                parts = []
                for k in range(COMPS):
                    total = None
                    for j in range(CDIM // 8):
                        u = user_pairs[c * CDIM + j * 8 : c * CDIM + (j + 1) * 8, span]
                        v = item_pairs[k * CDIM + j * 8 : k * CDIM + (j + 1) * 8, span]
                        total = u * v if total is None else total + u * v
                    parts.append(total)
                logits_ref[c * COMPS : (c + 1) * COMPS, span] = fold_rows(parts) * scale

    def gate(block):
        lanes = slice(block * WIDE, (block + 1) * WIDE)
        logits = logits_ref[:, lanes]
        pre = dot(w_in_fwd[...], value_stack(logits, True))
        sig = 0.5 * jnp.tanh(0.5 * pre) + 0.5
        hidden = pre * sig
        raw = dot(w_out_fwd[...], value_stack(hidden, True))
        capped = jnp.tanh(raw * (1.0 / gate_cap))
        powers = jnp.exp(gate_cap * capped)
        weights = powers * (1.0 / jnp.sum(powers, axis=0, keepdims=True))
        student = jnp.sum(weights * logits, axis=0, keepdims=True)
        residual = (student - target[:, lanes]) * (loss_scale * scale)
        d_gate = weights * (logits - student) * (1.0 - capped * capped)
        d_hidden = dot(w_out_bwd[...], value_stack(d_gate, False))
        d_pre = d_hidden * (sig + hidden * (1.0 - sig))
        d_flat = residual * (weights + dot(w_in_bwd[...], value_stack(d_pre, False)))
        grad_ref[:, lanes] = d_flat.astype(BF16).astype(F32)

    def gradients(block):
        for span in spans(block):
            pair_gradients(grad_ref, item_pairs, user_terms, span, lambda c, k: c * COMPS + k)

    stages = (gather, make_logits, gate, gradients)
    for step in range(blocks + len(stages) - 1):
        for at, stage in enumerate(stages):
            if 0 <= step - at < blocks:
                stage(step - at)
    collect(user_hot, user_terms, user_keep_ref, user_send_ref)


def item_kernel(user_pairs, item_hot, grad_ref, item_keep_ref, item_send_ref, item_terms):
    for at in range(0, item_hot.shape[1], TILE):
        pair_gradients(grad_ref, user_pairs, item_terms, slice(at, at + TILE), lambda k, c: c * COMPS + k)
    collect(item_hot, item_terms, item_keep_ref, item_send_ref)


def shape(rows, columns, kind):
    return jax.ShapeDtypeStruct((rows, columns), kind)


def call(kernel, outputs, scratch, arguments, grant, micros):
    return pl.pallas_call(
        kernel,
        out_shape=outputs,
        in_specs=[VMEM] * len(arguments),
        out_specs=[VMEM] * len(outputs),
        scratch_shapes=[pltpu.VMEM(s.shape, s.dtype) for s in scratch],
        compiler_params=pltpu.CompilerParams(vmem_limit_bytes=grant << 20),
        cost_estimate=pl.CostEstimate(flops=int(micros*5e8), bytes_accessed=int(micros * 3e6), transcendentals=0),
    )(*arguments)


def gather_round(value, axis, step):
    return jnp.concatenate([value, exchange(value, axis, step)], axis=0)


def local(user_comps, item_text, item_proj, w_in, b_in, w_out, b_out, pair_user, pair_item, teacher):
    n_user, n_item = lax.axis_size("user"), lax.axis_size("item")
    pairs, width = pair_user.shape[0], COMPS * CDIM
    hidden, gates = b_in.shape[0], b_out.shape[0]
    user_rows, item_rows = user_comps.shape[0] * n_item, item_text.shape[0] * n_user
    loss_scale = 2.0 * math.sqrt(user_rows / (pairs * n_item))

    (ready,) = call(ready_kernel, [shape(8, 128, F32)], [], [], 1, 8.0)
    users = user_comps
    for step in round_steps(n_item):
        users = gather_round(users, "item", step)
    (items,) = call(project_kernel, [shape(item_text.shape[0], width, BF16)], [], [item_text, item_proj, ready], 8, 2.0)
    for step in round_steps(n_user):
        items = gather_round(items, "user", step)

    user_pairs, user_hot, item_hot, w_in_fwd, w_out_fwd, w_in_bwd, w_out_bwd, target = call(
        functools.partial(user_kernel, (n_user, n_item)),
        [
            shape(width, pairs, F32),
            shape(user_rows, pairs, BF16),
            shape(item_rows, pairs, BF16),
            shape(hidden, 3 * gates + 16, BF16),
            shape(gates, 3 * hidden + 16, BF16),
            shape(gates, 3 * hidden, BF16),
            shape(hidden, 3 * gates, BF16),
            shape(1, pairs, F32),
        ],
        [],
        [
            users,
            w_in,
            b_in.reshape(1, -1),
            w_out,
            b_out.reshape(1, -1),
            pair_user.reshape(1, -1),
            pair_item.reshape(1, -1),
            teacher.reshape(1, -1),
        ],
        12,
        1.5,
    )
    user_keep, user_send, grads = call(
        functools.partial(pair_kernel, loss_scale),
        [shape(user_rows // 2, width, F32), shape(user_rows // 2, width, BF16), shape(gates, pairs, F32)],
        [shape(width, pairs, F32), shape(gates, pairs, F32), shape(width, pairs, BF16)],
        [items, user_pairs, user_hot, item_hot, w_in_fwd, w_out_fwd, w_in_bwd, w_out_bwd, target],
        20,
        4.5,
    )
    item_keep, item_send = call(
        item_kernel,
        [shape(item_rows // 2, width, F32), shape(item_rows // 2, width, BF16)],
        [shape(width, pairs, BF16)],
        [user_pairs, item_hot, grads],
        12,
        2.0,
    )

    def scatter(keep, send, axis):
        steps = round_steps(lax.axis_size(axis))[::-1]
        for at, step in enumerate(steps):
            total = keep + exchange(send, axis, step).astype(F32)
            if at + 1 < len(steps):
                half = total.shape[0] // 2
                keep, send = total[:half], total[half:].astype(BF16)
        return total

    return scatter(user_keep, user_send, "item"), scatter(item_keep, item_send, "user")


def solution(mesh):
    split = P(("user", "item"))
    rows = P(("user", "item"), None)
    in_specs = (rows, rows, P(), P(), P(), P(), P(), split, split, split)

    return jax.shard_map(local, mesh=mesh, in_specs=in_specs, out_specs=(rows, rows), check_vma=False)
```

```python
import functools
import math

import jax
import jax.numpy as jnp
from jax import lax
from jax.experimental import pallas as pl
from jax.experimental.pallas import tpu as pltpu
from jax.sharding import PartitionSpec as P


COMPS = 8
CDIM = 64
gate_cap = 8.0
F32 = jnp.float32
BF16 = jnp.bfloat16
VMEM = pl.BlockSpec(memory_space=pltpu.VMEM)
WIDE = 256
TILE = 128


def bits_of(size):
    return size.bit_length() - 1


def exchange(value, axis, step):
    size = lax.axis_size(axis)
    return lax.ppermute(value, axis, [(i, i ^ step) for i in range(size)])


def round_steps(size, crossed):
    steps = [(1 << bit) | crossed for bit in range(1, bits_of(size))]
    return steps + ([1] if size > 1 else [])


def place_of(block, me, size, crossed):
    apart = block ^ me
    bits = bits_of(size)
    if bits < 2:
        return apart
    last = apart & 1
    if crossed:
        for bit in range(1, bits):
            last = last ^ ((apart >> bit) & 1)
    return (apart >> 1) | (last << (bits - 1))


def ready_kernel(out_ref):
    out_ref[...] = jnp.zeros_like(out_ref)


def project_kernel(text_ref, proj_ref, ready_ref, out_ref):
    mixed = jnp.dot(text_ref[...], proj_ref[...], preferred_element_type=F32)
    parts = []
    for at in range(COMPS):
        part = mixed[:, at * CDIM : (at + 1) * CDIM]
        square = jnp.mean(part * part, axis=-1, keepdims=True)
        parts.append(part * lax.rsqrt(square + 1e-06))
    out_ref[...] = jnp.concatenate(parts, axis=1).astype(BF16)


def halves(value):
    upper = value.astype(BF16)
    return upper, (value - upper.astype(F32)).astype(BF16)


def weight_stack(weight, axis):
    upper, lower = halves(weight)
    return jnp.concatenate([upper, lower, upper], axis=axis)


def value_stack(value, bias):
    upper, lower = halves(value)
    pieces = [upper, upper, lower]
    if bias:
        pieces.append(jnp.ones((16, value.shape[1]), BF16))
    return jnp.concatenate(pieces, axis=0)


def bias_rows(bias):
    upper, rest = bias.astype(BF16), bias
    rows = [upper]
    for _ in range(2):
        rest = rest - upper.astype(F32)
        upper = rest.astype(BF16)
        rows.append(upper)
    rows.append(jnp.zeros((13, bias.shape[1]), BF16))
    return jnp.concatenate([r.astype(F32) for r in rows], axis=0).astype(BF16)


def fold_rows(parts):
    place = lax.broadcasted_iota(jnp.int32, parts[0].shape, 0)
    width = 4
    while len(parts) > 1:
        low = (place & width) == 0
        half = len(parts) // 2
        merged = []
        for at in range(half):
            one, two = parts[at], parts[at + half]
            stay = jnp.where(low, one, two)
            move = jnp.where(low, two, one)
            merged.append(stay + pltpu.roll(move, width, 0) if width == 4 else stay + shift_rows(move, width, low))
        parts = merged
        width //= 2
    return parts[0]


def shift_rows(value, width, low):
    return jnp.where(low, pltpu.roll(value, 8 - width, 0), pltpu.roll(value, width, 0))


def dot(one, two):
    return jnp.dot(one, two, preferred_element_type=F32)


def hot_rows(index, rows, size, me, crossed):
    each = rows // size
    spot = place_of(index // each, me, size, crossed) * each + index % each
    hot = lax.broadcasted_iota(jnp.int32, (rows, index.shape[1]), 0) == spot
    return jnp.where(hot, 1.0, 0.0).astype(BF16)


def item_kernel(
    sizes,
    items_ref,
    w_in_ref,
    b_in_ref,
    w_out_ref,
    b_out_ref,
    pair_user_ref,
    pair_item_ref,
    teacher_ref,
    item_pairs,
    user_hot,
    item_hot,
    w_in_fwd,
    w_out_fwd,
    w_in_bwd,
    w_out_bwd,
    target,
):
    n_user, n_item = sizes
    user_rows, item_rows = user_hot.shape[0], item_hot.shape[0]
    me_user, me_item = lax.axis_index("user"), lax.axis_index("item")
    w_in, w_out = w_in_ref[...], w_out_ref[...]
    w_in_fwd[...] = jnp.concatenate([weight_stack(w_in, 0), bias_rows(b_in_ref[...])], axis=0).T
    w_out_fwd[...] = jnp.concatenate([weight_stack(w_out, 0), bias_rows(b_out_ref[...])], axis=0).T
    w_in_bwd[...] = weight_stack(w_in, 1)
    w_out_bwd[...] = weight_stack(w_out, 1)
    target[...] = teacher_ref[...]
    items_t = items_ref[...].T
    for block in range(user_hot.shape[1] // WIDE):
        lanes = slice(block * WIDE, (block + 1) * WIDE)
        hot = hot_rows(pair_item_ref[:, lanes], item_rows, n_user, me_user, 1)
        item_hot[:, lanes] = hot
        item_pairs[:, lanes] = dot(items_t, hot)
        user_hot[:, lanes] = hot_rows(pair_user_ref[:, lanes], user_rows, n_item, me_item, 0)


def pair_gradients(grad_ref, pairs_ref, terms, span, row):
    for one in range(COMPS):
        spread = [
            jnp.broadcast_to(grad_ref[row(one, two) : row(one, two) + 1, span], (16, TILE)) for two in range(COMPS)
        ]
        for j in range(CDIM // 16):
            total = None
            for two in range(COMPS):
                at = two * CDIM + j * 16
                term = spread[two] * pairs_ref[at : at + 16, span]
                total = term if total is None else total + term
            at = one * CDIM + j * 16
            terms[at : at + 16, span] = total.astype(BF16)


def collect(hot, terms, keep_ref, send_ref):
    total = lax.dot_general(hot[...], terms[...], (((1,), (1,)), ((), ())), preferred_element_type=F32)
    half = total.shape[0] // 2
    keep_ref[...] = total[:half]
    send_ref[...] = total[half:].astype(BF16)


def pair_kernel(
    loss_scale,
    users_ref,
    item_pairs,
    user_hot,
    item_hot,
    w_in_fwd,
    w_out_fwd,
    w_in_bwd,
    w_out_bwd,
    target,
    item_keep_ref,
    item_send_ref,
    grad_ref,
    user_pairs,
    logits_ref,
    item_terms,
):
    pairs = user_hot.shape[1]
    blocks = pairs // WIDE
    scale = 1.0 / math.sqrt(CDIM)
    users_t = users_ref[...].T

    def gather(block):
        lanes = slice(block * WIDE, (block + 1) * WIDE)
        user_pairs[:, lanes] = dot(users_t, user_hot[:, lanes])

    def spans(block):
        return [slice(block * WIDE + at, block * WIDE + at + TILE) for at in range(0, WIDE, TILE)]

    def make_logits(block):
        for span in spans(block):
            for c in range(COMPS):
                parts = []
                for k in range(COMPS):
                    total = None
                    for j in range(CDIM // 8):
                        u = user_pairs[c * CDIM + j * 8 : c * CDIM + (j + 1) * 8, span]
                        v = item_pairs[k * CDIM + j * 8 : k * CDIM + (j + 1) * 8, span]
                        total = u * v if total is None else total + u * v
                    parts.append(total)
                logits_ref[c * COMPS : (c + 1) * COMPS, span] = fold_rows(parts) * scale

    def gate(block):
        lanes = slice(block * WIDE, (block + 1) * WIDE)
        logits = logits_ref[:, lanes]
        pre = dot(w_in_fwd[...], value_stack(logits, True))
        sig = 0.5 * jnp.tanh(0.5 * pre) + 0.5
        hidden = pre * sig
        raw = dot(w_out_fwd[...], value_stack(hidden, True))
        capped = jnp.tanh(raw * (1.0 / gate_cap))
        powers = jnp.exp(gate_cap * capped)
        weights = powers * (1.0 / jnp.sum(powers, axis=0, keepdims=True))
        student = jnp.sum(weights * logits, axis=0, keepdims=True)
        residual = (student - target[:, lanes]) * (loss_scale * scale)
        d_gate = weights * (logits - student) * (1.0 - capped * capped)
        d_hidden = dot(w_out_bwd[...], value_stack(d_gate, False))
        d_pre = d_hidden * (sig + hidden * (1.0 - sig))
        d_flat = residual * (weights + dot(w_in_bwd[...], value_stack(d_pre, False)))
        grad_ref[:, lanes] = d_flat.astype(BF16).astype(F32)

    def gradients(block):
        for span in spans(block):
            pair_gradients(grad_ref, user_pairs, item_terms, span, lambda k, c: c * COMPS + k)

    stages = (gather, make_logits, gate, gradients)
    for step in range(blocks + len(stages) - 1):
        for at, stage in enumerate(stages):
            if 0 <= step - at < blocks:
                stage(step - at)
    collect(item_hot, item_terms, item_keep_ref, item_send_ref)


def user_kernel(item_pairs, user_hot, grad_ref, user_keep_ref, user_send_ref, user_terms):
    for at in range(0, user_hot.shape[1], TILE):
        pair_gradients(grad_ref, item_pairs, user_terms, slice(at, at + TILE), lambda c, k: c * COMPS + k)
    collect(user_hot, user_terms, user_keep_ref, user_send_ref)


def shape(rows, columns, kind):
    return jax.ShapeDtypeStruct((rows, columns), kind)


def call(kernel, outputs, scratch, arguments, grant, micros):
    return pl.pallas_call(
        kernel,
        out_shape=outputs,
        in_specs=[VMEM] * len(arguments),
        out_specs=[VMEM] * len(outputs),
        scratch_shapes=[pltpu.VMEM(s.shape, s.dtype) for s in scratch],
        compiler_params=pltpu.CompilerParams(vmem_limit_bytes=grant << 20),
        cost_estimate=pl.CostEstimate(flops=int(micros*5e8), bytes_accessed=int(micros * 3e6), transcendentals=0),
    )(*arguments)


def gather_round(value, axis, step):
    return jnp.concatenate([value, exchange(value, axis, step)], axis=0)


def local(user_comps, item_text, item_proj, w_in, b_in, w_out, b_out, pair_user, pair_item, teacher):
    n_user, n_item = lax.axis_size("user"), lax.axis_size("item")
    pairs, width = pair_user.shape[0], COMPS * CDIM
    hidden, gates = b_in.shape[0], b_out.shape[0]
    user_rows, item_rows = user_comps.shape[0] * n_item, item_text.shape[0] * n_user
    loss_scale = 2.0 * math.sqrt(user_rows / (pairs * n_item))

    (ready,) = call(ready_kernel, [shape(8, 128, F32)], [], [], 1, 8.0)
    users = user_comps
    for step in round_steps(n_item, 0):
        users = gather_round(users, "item", step)
    (items,) = call(project_kernel, [shape(item_text.shape[0], width, BF16)], [], [item_text, item_proj, ready], 8, 2.0)
    for step in round_steps(n_user, 1):
        items = gather_round(items, "user", step)

    item_pairs, user_hot, item_hot, w_in_fwd, w_out_fwd, w_in_bwd, w_out_bwd, target = call(
        functools.partial(item_kernel, (n_user, n_item)),
        [
            shape(width, pairs, F32),
            shape(user_rows, pairs, BF16),
            shape(item_rows, pairs, BF16),
            shape(hidden, 3 * gates + 16, BF16),
            shape(gates, 3 * hidden + 16, BF16),
            shape(gates, 3 * hidden, BF16),
            shape(hidden, 3 * gates, BF16),
            shape(1, pairs, F32),
        ],
        [],
        [
            items,
            w_in,
            b_in.reshape(1, -1),
            w_out,
            b_out.reshape(1, -1),
            pair_user.reshape(1, -1),
            pair_item.reshape(1, -1),
            teacher.reshape(1, -1),
        ],
        12,
        1.5,
    )
    item_keep, item_send, grads = call(
        functools.partial(pair_kernel, loss_scale),
        [shape(item_rows // 2, width, F32), shape(item_rows // 2, width, BF16), shape(gates, pairs, F32)],
        [shape(width, pairs, F32), shape(gates, pairs, F32), shape(width, pairs, BF16)],
        [users, item_pairs, user_hot, item_hot, w_in_fwd, w_out_fwd, w_in_bwd, w_out_bwd, target],
        20,
        4.5,
    )
    user_keep, user_send = call(
        user_kernel,
        [shape(user_rows // 2, width, F32), shape(user_rows // 2, width, BF16)],
        [shape(width, pairs, BF16)],
        [item_pairs, user_hot, grads],
        12,
        2.0,
    )

    def scatter(keep, send, axis, crossed):
        steps = round_steps(lax.axis_size(axis), crossed)[::-1]
        for at, step in enumerate(steps):
            got = exchange(send, axis, step)
            total = keep + got.astype(F32)
            if at + 1 < len(steps):
                half = total.shape[0] // 2
                keep, send = total[:half], total[half:].astype(BF16)
        return total

    return scatter(user_keep, user_send, "item", 0), scatter(item_keep, item_send, "user", 1)


def solution(mesh):
    split = P(("user", "item"))
    rows = P(("user", "item"), None)
    in_specs = (rows, rows, P(), P(), P(), P(), P(), split, split, split)

    return jax.shard_map(local, mesh=mesh, in_specs=in_specs, out_specs=(rows, rows), check_vma=False)
```

```python
import functools
import math

import jax
import jax.numpy as jnp
from jax import lax
from jax.experimental import pallas as pl
from jax.experimental.pallas import tpu as pltpu
from jax.sharding import PartitionSpec as P


COMPS = 8
CDIM = 64
gate_cap = 8.0
F32 = jnp.float32
BF16 = jnp.bfloat16
VMEM = pl.BlockSpec(memory_space=pltpu.VMEM)
WIDE = 256
TILE = 128


def bits_of(size):
    return size.bit_length() - 1


def exchange(value, axis, step):
    size = lax.axis_size(axis)
    return lax.ppermute(value, axis, [(i, i ^ step) for i in range(size)])


def round_steps(size, crossed):
    steps = [(1 << bit) | crossed for bit in range(1, bits_of(size))]
    return steps + ([1] if size > 1 else [])


def place_of(block, me, size, crossed):
    apart = block ^ me
    bits = bits_of(size)
    if bits < 2:
        return apart
    last = apart & 1
    if crossed:
        for bit in range(1, bits):
            last = last ^ ((apart >> bit) & 1)
    return (apart >> 1) | (last << (bits - 1))


def ready_kernel(out_ref):
    out_ref[...] = jnp.zeros_like(out_ref)


def project_kernel(text_ref, proj_ref, ready_ref, out_ref):
    mixed = jnp.dot(text_ref[...], proj_ref[...], preferred_element_type=F32)
    parts = []
    for at in range(COMPS):
        part = mixed[:, at * CDIM : (at + 1) * CDIM]
        square = jnp.mean(part * part, axis=-1, keepdims=True)
        parts.append(part * lax.rsqrt(square + 1e-06))
    out_ref[...] = jnp.concatenate(parts, axis=1).astype(BF16)


def halves(value):
    upper = value.astype(BF16)
    return upper, (value - upper.astype(F32)).astype(BF16)


def weight_stack(weight, axis):
    upper, lower = halves(weight)
    return jnp.concatenate([upper, lower, upper], axis=axis)


def value_stack(value, bias):
    upper, lower = halves(value)
    pieces = [upper, upper, lower]
    if bias:
        pieces.append(jnp.ones((16, value.shape[1]), BF16))
    return jnp.concatenate(pieces, axis=0)


def bias_rows(bias):
    upper, rest = bias.astype(BF16), bias
    rows = [upper]
    for _ in range(2):
        rest = rest - upper.astype(F32)
        upper = rest.astype(BF16)
        rows.append(upper)
    rows.append(jnp.zeros((13, bias.shape[1]), BF16))
    return jnp.concatenate([r.astype(F32) for r in rows], axis=0).astype(BF16)


def fold_rows(parts):
    place = lax.broadcasted_iota(jnp.int32, parts[0].shape, 0)

    def merge(one, two, start, width):
        mine = ((place - start) & (2 * width - 1)) < width
        stay = jnp.where(mine, two, one)
        move = jnp.where(mine, one, two)
        return stay + pltpu.roll(move, width, 0)

    def quad(shift):
        first = merge(parts[(7 + shift) % 8], parts[(3 + shift) % 8], shift, 4)
        second = merge(parts[(1 + shift) % 8], parts[(5 + shift) % 8], 2 + shift, 4)
        return merge(first, second, 4 + shift, 2)

    return merge(quad(0), quad(1), 0, 1)


def dot(one, two):
    return jnp.dot(one, two, preferred_element_type=F32)


def hot_rows(index, rows, size, me, crossed):
    each = rows // size
    spot = place_of(index // each, me, size, crossed) * each + index % each
    hot = lax.broadcasted_iota(jnp.int32, (rows, index.shape[1]), 0) == spot
    return jnp.where(hot, 1.0, 0.0).astype(BF16)


def item_kernel(
    sizes,
    items_ref,
    w_in_ref,
    b_in_ref,
    w_out_ref,
    b_out_ref,
    pair_user_ref,
    pair_item_ref,
    teacher_ref,
    item_pairs,
    user_hot,
    item_hot,
    w_in_fwd,
    w_out_fwd,
    w_in_bwd,
    w_out_bwd,
    target,
):
    n_user, n_item = sizes
    user_rows, item_rows = user_hot.shape[0], item_hot.shape[0]
    me_user, me_item = lax.axis_index("user"), lax.axis_index("item")
    w_in, w_out = w_in_ref[...], w_out_ref[...]
    w_in_fwd[...] = jnp.concatenate([weight_stack(w_in, 0), bias_rows(b_in_ref[...])], axis=0).T
    w_out_fwd[...] = jnp.concatenate([weight_stack(w_out, 0), bias_rows(b_out_ref[...])], axis=0).T
    w_in_bwd[...] = weight_stack(w_in, 1)
    w_out_bwd[...] = weight_stack(w_out, 1)
    target[...] = teacher_ref[...]
    items_t = items_ref[...].T
    for block in range(user_hot.shape[1] // WIDE):
        lanes = slice(block * WIDE, (block + 1) * WIDE)
        hot = hot_rows(pair_item_ref[:, lanes], item_rows, n_user, me_user, 1)
        item_hot[:, lanes] = hot
        item_pairs[:, lanes] = dot(items_t, hot)
        user_hot[:, lanes] = hot_rows(pair_user_ref[:, lanes], user_rows, n_item, me_item, 0)


def pair_gradients(grad_ref, pairs_ref, terms, span, row):
    for one in range(COMPS):
        spread = [
            jnp.broadcast_to(grad_ref[row(one, two) : row(one, two) + 1, span], (16, TILE)) for two in range(COMPS)
        ]
        for j in range(CDIM // 16):
            total = None
            for two in range(COMPS):
                at = two * CDIM + j * 16
                term = spread[two] * pairs_ref[at : at + 16, span]
                total = term if total is None else total + term
            at = one * CDIM + j * 16
            terms[at : at + 16, span] = total.astype(BF16)


def collect(hot, terms, keep_ref, send_ref):
    total = lax.dot_general(hot[...], terms[...], (((1,), (1,)), ((), ())), preferred_element_type=F32)
    half = total.shape[0] // 2
    keep_ref[...] = total[:half]
    send_ref[...] = total[half:].astype(BF16)


def pair_kernel(
    loss_scale,
    users_ref,
    item_pairs,
    user_hot,
    item_hot,
    w_in_fwd,
    w_out_fwd,
    w_in_bwd,
    w_out_bwd,
    target,
    item_keep_ref,
    item_send_ref,
    grad_ref,
    user_pairs,
    logits_ref,
    item_terms,
):
    pairs = user_hot.shape[1]
    blocks = pairs // WIDE
    scale = 1.0 / math.sqrt(CDIM)
    users_t = users_ref[...].T

    def gather(block):
        lanes = slice(block * WIDE, (block + 1) * WIDE)
        user_pairs[:, lanes] = dot(users_t, user_hot[:, lanes])

    def spans(block):
        return [slice(block * WIDE + at, block * WIDE + at + TILE) for at in range(0, WIDE, TILE)]

    def make_logits(block):
        for span in spans(block):
            for c in range(0, COMPS, 2):
                parts = [[], []]
                for k in range(COMPS):
                    total = [None, None]
                    for j in range(CDIM // 8):
                        v = item_pairs[k * CDIM + j * 8 : k * CDIM + (j + 1) * 8, span]
                        for at in range(2):
                            row = (c + at) * CDIM + j * 8
                            term = user_pairs[row : row + 8, span] * v
                            total[at] = term if total[at] is None else total[at] + term
                    for at in range(2):
                        parts[at].append(total[at])
                for at in range(2):
                    row = (c + at) * COMPS
                    logits_ref[row : row + COMPS, span] = fold_rows(parts[at]) * scale

    def gate(block):
        lanes = slice(block * WIDE, (block + 1) * WIDE)
        logits = logits_ref[:, lanes]
        pre = dot(w_in_fwd[...], value_stack(logits, True))
        sig = 0.5 * jnp.tanh(0.5 * pre) + 0.5
        hidden = pre * sig
        raw = dot(w_out_fwd[...], value_stack(hidden, True))
        capped = jnp.tanh(raw * (1.0 / gate_cap))
        powers = jnp.exp(gate_cap * capped)
        weights = powers * (1.0 / jnp.sum(powers, axis=0, keepdims=True))
        student = jnp.sum(weights * logits, axis=0, keepdims=True)
        residual = (student - target[:, lanes]) * (loss_scale * scale)
        d_gate = weights * (logits - student) * (1.0 - capped * capped)
        d_hidden = dot(w_out_bwd[...], value_stack(d_gate, False))
        d_pre = d_hidden * (sig + hidden * (1.0 - sig))
        d_flat = residual * (weights + dot(w_in_bwd[...], value_stack(d_pre, False)))
        grad_ref[:, lanes] = d_flat.astype(BF16).astype(F32)

    def gradients(block):
        for span in spans(block):
            pair_gradients(grad_ref, user_pairs, item_terms, span, lambda k, c: c * COMPS + k)

    for block in range(blocks):
        gather(block)
    stages = (make_logits, gate, gradients)
    for step in range(blocks + len(stages) - 1):
        for at, stage in enumerate(stages):
            if 0 <= step - at < blocks:
                stage(step - at)
    collect(item_hot, item_terms, item_keep_ref, item_send_ref)


def user_kernel(item_pairs, user_hot, grad_ref, user_keep_ref, user_send_ref, user_terms):
    for at in range(0, user_hot.shape[1], TILE):
        pair_gradients(grad_ref, item_pairs, user_terms, slice(at, at + TILE), lambda c, k: c * COMPS + k)
    collect(user_hot, user_terms, user_keep_ref, user_send_ref)


def shape(rows, columns, kind):
    return jax.ShapeDtypeStruct((rows, columns), kind)


def call(kernel, outputs, scratch, arguments, grant, micros):
    return pl.pallas_call(
        kernel,
        out_shape=outputs,
        in_specs=[VMEM] * len(arguments),
        out_specs=[VMEM] * len(outputs),
        scratch_shapes=[pltpu.VMEM(s.shape, s.dtype) for s in scratch],
        compiler_params=pltpu.CompilerParams(vmem_limit_bytes=grant << 20),
        cost_estimate=pl.CostEstimate(flops=int(micros*5e8), bytes_accessed=int(micros * 3e6), transcendentals=0),
    )(*arguments)


def gather_round(value, axis, step):
    return jnp.concatenate([value, exchange(value, axis, step)], axis=0)


def local(user_comps, item_text, item_proj, w_in, b_in, w_out, b_out, pair_user, pair_item, teacher):
    n_user, n_item = lax.axis_size("user"), lax.axis_size("item")
    pairs, width = pair_user.shape[0], COMPS * CDIM
    hidden, gates = b_in.shape[0], b_out.shape[0]
    user_rows, item_rows = user_comps.shape[0] * n_item, item_text.shape[0] * n_user
    loss_scale = 2.0 * math.sqrt(user_rows / (pairs * n_item))

    (ready,) = call(ready_kernel, [shape(8, 128, F32)], [], [], 1, 8.0)
    users = user_comps
    for step in round_steps(n_item, 0):
        users = gather_round(users, "item", step)
    (items,) = call(project_kernel, [shape(item_text.shape[0], width, BF16)], [], [item_text, item_proj, ready], 8, 2.0)
    for step in round_steps(n_user, 1):
        items = gather_round(items, "user", step)

    item_pairs, user_hot, item_hot, w_in_fwd, w_out_fwd, w_in_bwd, w_out_bwd, target = call(
        functools.partial(item_kernel, (n_user, n_item)),
        [
            shape(width, pairs, F32),
            shape(user_rows, pairs, BF16),
            shape(item_rows, pairs, BF16),
            shape(hidden, 3 * gates + 16, BF16),
            shape(gates, 3 * hidden + 16, BF16),
            shape(gates, 3 * hidden, BF16),
            shape(hidden, 3 * gates, BF16),
            shape(1, pairs, F32),
        ],
        [],
        [
            items,
            w_in,
            b_in.reshape(1, -1),
            w_out,
            b_out.reshape(1, -1),
            pair_user.reshape(1, -1),
            pair_item.reshape(1, -1),
            teacher.reshape(1, -1),
        ],
        12,
        1.5,
    )
    item_keep, item_send, grads = call(
        functools.partial(pair_kernel, loss_scale),
        [shape(item_rows // 2, width, F32), shape(item_rows // 2, width, BF16), shape(gates, pairs, F32)],
        [shape(width, pairs, F32), shape(gates, pairs, F32), shape(width, pairs, BF16)],
        [users, item_pairs, user_hot, item_hot, w_in_fwd, w_out_fwd, w_in_bwd, w_out_bwd, target],
        20,
        4.5,
    )
    user_keep, user_send = call(
        user_kernel,
        [shape(user_rows // 2, width, F32), shape(user_rows // 2, width, BF16)],
        [shape(width, pairs, BF16)],
        [item_pairs, user_hot, grads],
        12,
        2.0,
    )

    def scatter(keep, send, axis, crossed):
        steps = round_steps(lax.axis_size(axis), crossed)[::-1]
        for at, step in enumerate(steps):
            got = exchange(send, axis, step)
            total = keep + got.astype(F32)
            if at + 1 < len(steps):
                half = total.shape[0] // 2
                keep, send = total[:half], total[half:].astype(BF16)
        return total

    return scatter(user_keep, user_send, "item", 0), scatter(item_keep, item_send, "user", 1)


def solution(mesh):
    split = P(("user", "item"))
    rows = P(("user", "item"), None)
    in_specs = (rows, rows, P(), P(), P(), P(), P(), split, split, split)

    return jax.shard_map(local, mesh=mesh, in_specs=in_specs, out_specs=(rows, rows), check_vma=False)
```

```python
import functools
import math

import jax
import jax.numpy as jnp
from jax import lax
from jax.experimental import pallas as pl
from jax.experimental.pallas import tpu as pltpu
from jax.sharding import PartitionSpec as P


COMPS = 8
CDIM = 64
gate_cap = 8.0
F32 = jnp.float32
BF16 = jnp.bfloat16
VMEM = pl.BlockSpec(memory_space=pltpu.VMEM)
WIDE = 256
TILE = 128


def bits_of(size):
    return size.bit_length() - 1


def exchange(value, axis, step):
    size = lax.axis_size(axis)
    return lax.ppermute(value, axis, [(i, i ^ step) for i in range(size)])


def round_steps(size, crossed):
    steps = [(1 << bit) | crossed for bit in range(1, bits_of(size))]
    return steps + ([1] if size > 1 else [])


def place_of(block, me, size, crossed):
    apart = block ^ me
    bits = bits_of(size)
    if bits < 2:
        return apart
    last = apart & 1
    if crossed:
        for bit in range(1, bits):
            last = last ^ ((apart >> bit) & 1)
    return (apart >> 1) | (last << (bits - 1))


def ready_kernel(out_ref):
    out_ref[...] = jnp.zeros_like(out_ref)


def project_kernel(text_ref, proj_ref, ready_ref, out_ref):
    mixed = jnp.dot(text_ref[...], proj_ref[...], preferred_element_type=F32)
    parts = []
    for at in range(COMPS):
        part = mixed[:, at * CDIM : (at + 1) * CDIM]
        square = jnp.mean(part * part, axis=-1, keepdims=True)
        parts.append(part * lax.rsqrt(square + 1e-06))
    out_ref[...] = jnp.concatenate(parts, axis=1).astype(BF16)


def halves(value):
    upper = value.astype(BF16)
    return upper, (value - upper.astype(F32)).astype(BF16)


def weight_stack(weight, axis):
    upper, lower = halves(weight)
    return jnp.concatenate([upper, lower, upper], axis=axis)


def value_stack(value, bias):
    upper, lower = halves(value)
    pieces = [upper, upper, lower]
    if bias:
        pieces.append(jnp.ones((16, value.shape[1]), BF16))
    return jnp.concatenate(pieces, axis=0)


def bias_rows(bias):
    upper, rest = bias.astype(BF16), bias
    rows = [upper]
    for _ in range(2):
        rest = rest - upper.astype(F32)
        upper = rest.astype(BF16)
        rows.append(upper)
    rows.append(jnp.zeros((13, bias.shape[1]), BF16))
    return jnp.concatenate([r.astype(F32) for r in rows], axis=0).astype(BF16)


def fold_rows(parts):
    place = lax.broadcasted_iota(jnp.int32, parts[0].shape, 0)

    def merge(one, two, start, width):
        mine = ((place - start) & (2 * width - 1)) < width
        stay = jnp.where(mine, two, one)
        move = jnp.where(mine, one, two)
        return stay + pltpu.roll(move, width, 0)

    def quad(shift):
        first = merge(parts[(7 + shift) % 8], parts[(3 + shift) % 8], shift, 4)
        second = merge(parts[(1 + shift) % 8], parts[(5 + shift) % 8], 2 + shift, 4)
        return merge(first, second, 4 + shift, 2)

    return merge(quad(0), quad(1), 0, 1)


def dot(one, two):
    return jnp.dot(one, two, preferred_element_type=F32)


def hot_rows(index, rows, size, me, crossed):
    each = rows // size
    spot = place_of(index // each, me, size, crossed) * each + index % each
    hot = lax.broadcasted_iota(jnp.int32, (rows, index.shape[1]), 0) == spot
    return jnp.where(hot, 1.0, 0.0).astype(BF16)


def item_kernel(
    sizes,
    items_ref,
    w_in_ref,
    b_in_ref,
    w_out_ref,
    b_out_ref,
    pair_user_ref,
    pair_item_ref,
    teacher_ref,
    item_pairs,
    item_short,
    user_hot,
    item_hot,
    w_in_fwd,
    w_out_fwd,
    w_in_bwd,
    w_out_bwd,
    target,
):
    n_user, n_item = sizes
    user_rows, item_rows = user_hot.shape[0], item_hot.shape[0]
    me_user, me_item = lax.axis_index("user"), lax.axis_index("item")
    w_in, w_out = w_in_ref[...], w_out_ref[...]
    w_in_fwd[...] = jnp.concatenate([weight_stack(w_in, 0), bias_rows(b_in_ref[...])], axis=0).T
    w_out_fwd[...] = jnp.concatenate([weight_stack(w_out, 0), bias_rows(b_out_ref[...])], axis=0).T
    w_in_bwd[...] = weight_stack(w_in, 1)
    w_out_bwd[...] = weight_stack(w_out, 1)
    target[...] = teacher_ref[...]
    items_t = items_ref[...].T
    for block in range(user_hot.shape[1] // WIDE):
        lanes = slice(block * WIDE, (block + 1) * WIDE)
        hot = hot_rows(pair_item_ref[:, lanes], item_rows, n_user, me_user, 1)
        item_hot[:, lanes] = hot
        rows = dot(items_t, hot)
        item_pairs[:, lanes] = rows
        for at in range(WIDE // TILE):
            item_short[block * (WIDE // TILE) + at] = rows[:, at * TILE : (at + 1) * TILE].astype(BF16)
        user_hot[:, lanes] = hot_rows(pair_user_ref[:, lanes], user_rows, n_item, me_item, 0)


def pair_gradients(grad_ref, pairs_ref, terms, span, row):
    for one in range(COMPS):
        spread = [
            jnp.broadcast_to(grad_ref[row(one, two) : row(one, two) + 1, span], (16, TILE)) for two in range(COMPS)
        ]
        for j in range(CDIM // 16):
            total = None
            for two in range(COMPS):
                at = two * CDIM + j * 16
                term = spread[two] * pairs_ref[at : at + 16, span]
                total = term if total is None else total + term
            at = one * CDIM + j * 16
            terms[at : at + 16, span] = total.astype(BF16)


def short_gradients(grad_ref, pairs_ref, terms, tile, row):
    span = slice(tile * TILE, (tile + 1) * TILE)
    for first in range(0, COMPS, 1):
        spread = [
            [
                jnp.broadcast_to(grad_ref[row(one, two) : row(one, two) + 1, span], (16, TILE)).astype(BF16)
                for two in range(COMPS)
            ]
            for one in range(first, first + 1)
        ]
        for j in range(CDIM // 16):
            values = []
            for two in range(COMPS):
                at = two * CDIM + j * 16
                values.append(pairs_ref[tile, at : at + 16, :])
            for one in range(1):
                parts = [spread[one][two] * values[two] for two in range(COMPS)]
                while len(parts) > 1:
                    parts = [parts[i] + parts[i + 1] for i in range(0, len(parts), 2)]
                at = (first + one) * CDIM + j * 16
                terms[at : at + 16, span] = parts[0]


def collect(hot, terms, keep_ref, send_ref):
    total = lax.dot_general(hot[...], terms[...], (((1,), (1,)), ((), ())), preferred_element_type=F32)
    half = total.shape[0] // 2
    keep_ref[...] = total[:half]
    send_ref[...] = total[half:].astype(BF16)


def pair_kernel(
    loss_scale,
    users_ref,
    item_pairs,
    user_hot,
    item_hot,
    w_in_fwd,
    w_out_fwd,
    w_in_bwd,
    w_out_bwd,
    target,
    item_keep_ref,
    item_send_ref,
    grad_ref,
    user_pairs,
    logits_ref,
    item_terms,
):
    pairs = user_hot.shape[1]
    blocks = pairs // WIDE
    scale = 1.0 / math.sqrt(CDIM)
    users_t = users_ref[...].T

    def gather(block):
        lanes = slice(block * WIDE, (block + 1) * WIDE)
        user_pairs[:, lanes] = dot(users_t, user_hot[:, lanes])

    def spans(block):
        return [slice(block * WIDE + at, block * WIDE + at + TILE) for at in range(0, WIDE, TILE)]

    def make_logits(block):
        for span in spans(block):
            for c in range(0, COMPS, 2):
                parts = [[], []]
                for k in range(COMPS):
                    total = [None, None]
                    for j in range(CDIM // 8):
                        v = item_pairs[k * CDIM + j * 8 : k * CDIM + (j + 1) * 8, span]
                        for at in range(2):
                            row = (c + at) * CDIM + j * 8
                            term = user_pairs[row : row + 8, span] * v
                            total[at] = term if total[at] is None else total[at] + term
                    for at in range(2):
                        parts[at].append(total[at])
                for at in range(2):
                    row = (c + at) * COMPS
                    logits_ref[row : row + COMPS, span] = fold_rows(parts[at]) * scale

    def gate(block):
        lanes = slice(block * WIDE, (block + 1) * WIDE)
        logits = logits_ref[:, lanes]
        pre = dot(w_in_fwd[...], value_stack(logits, True))
        sig = 0.5 * jnp.tanh(0.5 * pre) + 0.5
        hidden = pre * sig
        raw = dot(w_out_fwd[...], value_stack(hidden, True))
        capped = jnp.tanh(raw * (1.0 / gate_cap))
        powers = jnp.exp(gate_cap * capped)
        weights = powers * (1.0 / jnp.sum(powers, axis=0, keepdims=True))
        student = jnp.sum(weights * logits, axis=0, keepdims=True)
        residual = (student - target[:, lanes]) * (loss_scale * scale)
        d_gate = weights * (logits - student) * (1.0 - capped * capped)
        d_hidden = dot(w_out_bwd[...], value_stack(d_gate, False))
        d_pre = d_hidden * (sig + hidden * (1.0 - sig))
        d_flat = residual * (weights + dot(w_in_bwd[...], value_stack(d_pre, False)))
        grad_ref[:, lanes] = d_flat.astype(BF16).astype(F32)

    def gradients(block):
        for span in spans(block):
            pair_gradients(grad_ref, user_pairs, item_terms, span, lambda k, c: c * COMPS + k)

    for block in range(blocks):
        gather(block)
    stages = (make_logits, gate, gradients)
    for step in range(blocks + len(stages) - 1):
        for at, stage in enumerate(stages):
            if 0 <= step - at < blocks:
                stage(step - at)
    collect(item_hot, item_terms, item_keep_ref, item_send_ref)


def user_kernel(item_short, user_hot, grad_ref, user_keep_ref, user_send_ref, user_terms):
    for tile in range(user_hot.shape[1] // TILE):
        short_gradients(grad_ref, item_short, user_terms, tile, lambda c, k: c * COMPS + k)
    collect(user_hot, user_terms, user_keep_ref, user_send_ref)


def shape(rows, columns, kind):
    return jax.ShapeDtypeStruct((rows, columns), kind)


def call(kernel, outputs, scratch, arguments, grant, micros):
    return pl.pallas_call(
        kernel,
        out_shape=outputs,
        in_specs=[VMEM] * len(arguments),
        out_specs=[VMEM] * len(outputs),
        scratch_shapes=[pltpu.VMEM(s.shape, s.dtype) for s in scratch],
        compiler_params=pltpu.CompilerParams(vmem_limit_bytes=grant << 20),
        cost_estimate=pl.CostEstimate(flops=int(micros*5e8), bytes_accessed=int(micros * 3e6), transcendentals=0),
    )(*arguments)


def gather_round(value, axis, step):
    return jnp.concatenate([value, exchange(value, axis, step)], axis=0)


def local(user_comps, item_text, item_proj, w_in, b_in, w_out, b_out, pair_user, pair_item, teacher):
    n_user, n_item = lax.axis_size("user"), lax.axis_size("item")
    pairs, width = pair_user.shape[0], COMPS * CDIM
    hidden, gates = b_in.shape[0], b_out.shape[0]
    user_rows, item_rows = user_comps.shape[0] * n_item, item_text.shape[0] * n_user
    loss_scale = 2.0 * math.sqrt(user_rows / (pairs * n_item))

    (ready,) = call(ready_kernel, [shape(8, 128, F32)], [], [], 1, 8.0)
    users = user_comps
    for step in round_steps(n_item, 0):
        users = gather_round(users, "item", step)
    (items,) = call(project_kernel, [shape(item_text.shape[0], width, BF16)], [], [item_text, item_proj, ready], 8, 2.0)
    for step in round_steps(n_user, 1):
        items = gather_round(items, "user", step)

    item_pairs, item_short, user_hot, item_hot, w_in_fwd, w_out_fwd, w_in_bwd, w_out_bwd, target = call(
        functools.partial(item_kernel, (n_user, n_item)),
        [
            shape(width, pairs, F32),
            jax.ShapeDtypeStruct((pairs // TILE, width, TILE), BF16),
            shape(user_rows, pairs, BF16),
            shape(item_rows, pairs, BF16),
            shape(hidden, 3 * gates + 16, BF16),
            shape(gates, 3 * hidden + 16, BF16),
            shape(gates, 3 * hidden, BF16),
            shape(hidden, 3 * gates, BF16),
            shape(1, pairs, F32),
        ],
        [],
        [
            items,
            w_in,
            b_in.reshape(1, -1),
            w_out,
            b_out.reshape(1, -1),
            pair_user.reshape(1, -1),
            pair_item.reshape(1, -1),
            teacher.reshape(1, -1),
        ],
        12,
        1.5,
    )
    item_keep, item_send, grads = call(
        functools.partial(pair_kernel, loss_scale),
        [shape(item_rows // 2, width, F32), shape(item_rows // 2, width, BF16), shape(gates, pairs, F32)],
        [shape(width, pairs, F32), shape(gates, pairs, F32), shape(width, pairs, BF16)],
        [users, item_pairs, user_hot, item_hot, w_in_fwd, w_out_fwd, w_in_bwd, w_out_bwd, target],
        20,
        4.5,
    )
    user_keep, user_send = call(
        user_kernel,
        [shape(user_rows // 2, width, F32), shape(user_rows // 2, width, BF16)],
        [shape(width, pairs, BF16)],
        [item_short, user_hot, grads],
        12,
        2.0,
    )

    def scatter(keep, send, axis, crossed):
        steps = round_steps(lax.axis_size(axis), crossed)[::-1]
        for at, step in enumerate(steps):
            got = exchange(send, axis, step)
            total = keep + got.astype(F32)
            if at + 1 < len(steps):
                half = total.shape[0] // 2
                keep, send = total[:half], total[half:].astype(BF16)
        return total

    return scatter(user_keep, user_send, "item", 0), scatter(item_keep, item_send, "user", 1)


def solution(mesh):
    split = P(("user", "item"))
    rows = P(("user", "item"), None)
    in_specs = (rows, rows, P(), P(), P(), P(), P(), split, split, split)

    return jax.shard_map(local, mesh=mesh, in_specs=in_specs, out_specs=(rows, rows), check_vma=False)
```

```python
import functools
import math

import jax
import jax.numpy as jnp
from jax import lax
from jax.experimental import pallas as pl
from jax.experimental.pallas import tpu as pltpu
from jax.sharding import PartitionSpec as P


COMPS = 8
CDIM = 64
gate_cap = 8.0
F32 = jnp.float32
BF16 = jnp.bfloat16
VMEM = pl.BlockSpec(memory_space=pltpu.VMEM)
WIDE = 256
TILE = 128


def bits_of(size):
    return size.bit_length() - 1


def exchange(value, axis, step):
    size = lax.axis_size(axis)
    return lax.ppermute(value, axis, [(i, i ^ step) for i in range(size)])


def round_steps(size, crossed):
    steps = [(1 << bit) | crossed for bit in range(1, bits_of(size))]
    return steps + ([1] if size > 1 else [])


def place_of(block, me, size, crossed):
    apart = block ^ me
    bits = bits_of(size)
    if bits < 2:
        return apart
    last = apart & 1
    if crossed:
        for bit in range(1, bits):
            last = last ^ ((apart >> bit) & 1)
    return (apart >> 1) | (last << (bits - 1))


def ready_kernel(out_ref):
    out_ref[...] = jnp.zeros_like(out_ref)


def project_kernel(text_ref, proj_ref, ready_ref, out_ref):
    mixed = jnp.dot(text_ref[...], proj_ref[...], preferred_element_type=F32)
    parts = []
    for at in range(COMPS):
        part = mixed[:, at * CDIM : (at + 1) * CDIM]
        square = jnp.mean(part * part, axis=-1, keepdims=True)
        parts.append(part * lax.rsqrt(square + 1e-06))
    out_ref[...] = jnp.concatenate(parts, axis=1).astype(BF16)


def halves(value):
    upper = value.astype(BF16)
    return upper, (value - upper.astype(F32)).astype(BF16)


def weight_stack(weight, axis):
    upper, lower = halves(weight)
    return jnp.concatenate([upper, lower, upper], axis=axis)


def value_stack(value, bias):
    upper, lower = halves(value)
    pieces = [upper, upper, lower]
    if bias:
        pieces.append(jnp.ones((16, value.shape[1]), BF16))
    return jnp.concatenate(pieces, axis=0)


def bias_rows(bias):
    upper, rest = bias.astype(BF16), bias
    rows = [upper]
    for _ in range(2):
        rest = rest - upper.astype(F32)
        upper = rest.astype(BF16)
        rows.append(upper)
    rows.append(jnp.zeros((13, bias.shape[1]), BF16))
    return jnp.concatenate([r.astype(F32) for r in rows], axis=0).astype(BF16)


def fold_rows(parts):
    place = lax.broadcasted_iota(jnp.int32, parts[0].shape, 0)

    def merge(one, two, start, width):
        mine = ((place - start) & (2 * width - 1)) < width
        stay = jnp.where(mine, two, one)
        move = jnp.where(mine, one, two)
        return stay + pltpu.roll(move, width, 0)

    def quad(shift):
        first = merge(parts[(7 + shift) % 8], parts[(3 + shift) % 8], shift, 4)
        second = merge(parts[(1 + shift) % 8], parts[(5 + shift) % 8], 2 + shift, 4)
        return merge(first, second, 4 + shift, 2)

    return merge(quad(0), quad(1), 0, 1)


def dot(one, two):
    return jnp.dot(one, two, preferred_element_type=F32)


def hot_rows(index, rows, size, me, crossed):
    each = rows // size
    spot = place_of(index // each, me, size, crossed) * each + index % each
    hot = lax.broadcasted_iota(jnp.int32, (rows, index.shape[1]), 0) == spot
    return jnp.where(hot, 1.0, 0.0).astype(BF16)


def item_kernel(
    sizes,
    items_ref,
    w_in_ref,
    b_in_ref,
    w_out_ref,
    b_out_ref,
    pair_user_ref,
    pair_item_ref,
    teacher_ref,
    item_pairs,
    item_short,
    user_hot,
    item_hot,
    w_in_fwd,
    w_out_fwd,
    w_in_bwd,
    w_out_bwd,
    target,
):
    n_user, n_item = sizes
    user_rows, item_rows = user_hot.shape[0], item_hot.shape[0]
    me_user, me_item = lax.axis_index("user"), lax.axis_index("item")
    w_in, w_out = w_in_ref[...], w_out_ref[...]
    w_in_fwd[...] = jnp.concatenate([weight_stack(w_in, 0), bias_rows(b_in_ref[...])], axis=0).T
    w_out_fwd[...] = jnp.concatenate([weight_stack(w_out, 0), bias_rows(b_out_ref[...])], axis=0).T
    w_in_bwd[...] = weight_stack(w_in, 1)
    w_out_bwd[...] = weight_stack(w_out, 1)
    target[...] = teacher_ref[...]
    items_t = items_ref[...].T
    for block in range(user_hot.shape[1] // WIDE):
        lanes = slice(block * WIDE, (block + 1) * WIDE)
        hot = hot_rows(pair_item_ref[:, lanes], item_rows, n_user, me_user, 1)
        item_hot[:, lanes] = hot
        rows = dot(items_t, hot)
        item_pairs[:, lanes] = rows
        for at in range(WIDE // TILE):
            item_short[block * (WIDE // TILE) + at] = rows[:, at * TILE : (at + 1) * TILE].astype(BF16)
        user_hot[:, lanes] = hot_rows(pair_user_ref[:, lanes], user_rows, n_item, me_item, 0)


def pair_gradients(grad_ref, pairs_ref, terms, span, row):
    for one in range(COMPS):
        spread = [
            jnp.broadcast_to(grad_ref[row(one, two) : row(one, two) + 1, span], (16, TILE)) for two in range(COMPS)
        ]
        for j in range(CDIM // 16):
            total = None
            for two in range(COMPS):
                at = two * CDIM + j * 16
                term = spread[two] * pairs_ref[at : at + 16, span]
                total = term if total is None else total + term
            at = one * CDIM + j * 16
            terms[at : at + 16, span] = total.astype(BF16)


def short_gradients(grad_ref, pairs_ref, terms, tile, row):
    span = slice(tile * TILE, (tile + 1) * TILE)
    for first in range(0, COMPS, 1):
        spread = [
            [
                jnp.broadcast_to(grad_ref[row(one, two) : row(one, two) + 1, span], (16, TILE)).astype(BF16)
                for two in range(COMPS)
            ]
            for one in range(first, first + 1)
        ]
        for j in range(CDIM // 16):
            values = []
            for two in range(COMPS):
                at = two * CDIM + j * 16
                values.append(pairs_ref[tile, at : at + 16, :])
            for one in range(1):
                parts = [spread[one][two] * values[two] for two in range(COMPS)]
                while len(parts) > 1:
                    parts = [parts[i] + parts[i + 1] for i in range(0, len(parts), 2)]
                at = (first + one) * CDIM + j * 16
                terms[at : at + 16, span] = parts[0]


def collect(hot, terms):
    return lax.dot_general(hot, terms, (((1,), (1,)), ((), ())), preferred_element_type=F32)


def pair_kernel(
    loss_scale,
    users_ref,
    item_pairs,
    user_hot,
    item_hot,
    w_in_fwd,
    w_out_fwd,
    w_in_bwd,
    w_out_bwd,
    target,
    item_send_ref,
    grad_ref,
    item_terms,
    user_pairs,
    logits_ref,
):
    pairs = user_hot.shape[1]
    blocks = pairs // WIDE
    scale = 1.0 / math.sqrt(CDIM)
    users_t = users_ref[...].T

    def gather(block):
        lanes = slice(block * WIDE, (block + 1) * WIDE)
        user_pairs[:, lanes] = dot(users_t, user_hot[:, lanes])

    def spans(block):
        return [slice(block * WIDE + at, block * WIDE + at + TILE) for at in range(0, WIDE, TILE)]

    def make_logits(block):
        for span in spans(block):
            for c in range(0, COMPS, 2):
                parts = [[], []]
                for k in range(COMPS):
                    total = [None, None]
                    for j in range(CDIM // 8):
                        v = item_pairs[k * CDIM + j * 8 : k * CDIM + (j + 1) * 8, span]
                        for at in range(2):
                            row = (c + at) * CDIM + j * 8
                            term = user_pairs[row : row + 8, span] * v
                            total[at] = term if total[at] is None else total[at] + term
                    for at in range(2):
                        parts[at].append(total[at])
                for at in range(2):
                    row = (c + at) * COMPS
                    logits_ref[row : row + COMPS, span] = fold_rows(parts[at]) * scale

    def gate(block):
        lanes = slice(block * WIDE, (block + 1) * WIDE)
        logits = logits_ref[:, lanes]
        pre = dot(w_in_fwd[...], value_stack(logits, True))
        sig = 0.5 * jnp.tanh(0.5 * pre) + 0.5
        hidden = pre * sig
        raw = dot(w_out_fwd[...], value_stack(hidden, True))
        capped = jnp.tanh(raw * (1.0 / gate_cap))
        powers = jnp.exp(gate_cap * capped)
        weights = powers * (1.0 / jnp.sum(powers, axis=0, keepdims=True))
        student = jnp.sum(weights * logits, axis=0, keepdims=True)
        residual = (student - target[:, lanes]) * (loss_scale * scale)
        d_gate = weights * (logits - student) * (1.0 - capped * capped)
        d_hidden = dot(w_out_bwd[...], value_stack(d_gate, False))
        d_pre = d_hidden * (sig + hidden * (1.0 - sig))
        d_flat = residual * (weights + dot(w_in_bwd[...], value_stack(d_pre, False)))
        grad_ref[:, lanes] = d_flat.astype(BF16).astype(F32)

    def gradients(block):
        for span in spans(block):
            pair_gradients(grad_ref, user_pairs, item_terms, span, lambda k, c: c * COMPS + k)

    for block in range(blocks):
        gather(block)
    stages = (make_logits, gate, gradients)
    for step in range(blocks + len(stages) - 1):
        for at, stage in enumerate(stages):
            if 0 <= step - at < blocks:
                stage(step - at)
    half = item_hot.shape[0] // 2
    item_send_ref[...] = collect(item_hot[half:, :], item_terms[...]).astype(BF16)


def user_kernel(
    item_short, user_hot, grad_ref, item_hot, item_terms, user_keep_ref, user_send_ref, item_keep_ref, user_terms
):
    half = item_hot.shape[0] // 2
    item_keep_ref[...] = collect(item_hot[:half, :], item_terms[...])
    for tile in range(user_hot.shape[1] // TILE):
        short_gradients(grad_ref, item_short, user_terms, tile, lambda c, k: c * COMPS + k)
    total = collect(user_hot[...], user_terms[...])
    half = total.shape[0] // 2
    user_keep_ref[...] = total[:half]
    user_send_ref[...] = total[half:].astype(BF16)


def shape(rows, columns, kind):
    return jax.ShapeDtypeStruct((rows, columns), kind)


def call(kernel, outputs, scratch, arguments, grant, micros):
    return pl.pallas_call(
        kernel,
        out_shape=outputs,
        in_specs=[VMEM] * len(arguments),
        out_specs=[VMEM] * len(outputs),
        scratch_shapes=[pltpu.VMEM(s.shape, s.dtype) for s in scratch],
        compiler_params=pltpu.CompilerParams(vmem_limit_bytes=grant << 20),
        cost_estimate=pl.CostEstimate(flops=int(micros*5e8), bytes_accessed=int(micros * 3e6), transcendentals=0),
    )(*arguments)


def gather_round(value, axis, step):
    return jnp.concatenate([value, exchange(value, axis, step)], axis=0)


def local(user_comps, item_text, item_proj, w_in, b_in, w_out, b_out, pair_user, pair_item, teacher):
    n_user, n_item = lax.axis_size("user"), lax.axis_size("item")
    pairs, width = pair_user.shape[0], COMPS * CDIM
    hidden, gates = b_in.shape[0], b_out.shape[0]
    user_rows, item_rows = user_comps.shape[0] * n_item, item_text.shape[0] * n_user
    loss_scale = 2.0 * math.sqrt(user_rows / (pairs * n_item))

    (ready,) = call(ready_kernel, [shape(8, 128, F32)], [], [], 1, 8.0)
    users = user_comps
    for step in round_steps(n_item, 0):
        users = gather_round(users, "item", step)
    (items,) = call(project_kernel, [shape(item_text.shape[0], width, BF16)], [], [item_text, item_proj, ready], 8, 2.0)
    for step in round_steps(n_user, 1):
        items = gather_round(items, "user", step)

    item_pairs, item_short, user_hot, item_hot, w_in_fwd, w_out_fwd, w_in_bwd, w_out_bwd, target = call(
        functools.partial(item_kernel, (n_user, n_item)),
        [
            shape(width, pairs, F32),
            jax.ShapeDtypeStruct((pairs // TILE, width, TILE), BF16),
            shape(user_rows, pairs, BF16),
            shape(item_rows, pairs, BF16),
            shape(hidden, 3 * gates + 16, BF16),
            shape(gates, 3 * hidden + 16, BF16),
            shape(gates, 3 * hidden, BF16),
            shape(hidden, 3 * gates, BF16),
            shape(1, pairs, F32),
        ],
        [],
        [
            items,
            w_in,
            b_in.reshape(1, -1),
            w_out,
            b_out.reshape(1, -1),
            pair_user.reshape(1, -1),
            pair_item.reshape(1, -1),
            teacher.reshape(1, -1),
        ],
        12,
        1.5,
    )
    item_send, grads, item_terms = call(
        functools.partial(pair_kernel, loss_scale),
        [shape(item_rows // 2, width, BF16), shape(gates, pairs, F32), shape(width, pairs, BF16)],
        [shape(width, pairs, F32), shape(gates, pairs, F32)],
        [users, item_pairs, user_hot, item_hot, w_in_fwd, w_out_fwd, w_in_bwd, w_out_bwd, target],
        20,
        4.5,
    )
    user_keep, user_send, item_keep = call(
        user_kernel,
        [
            shape(user_rows // 2, width, F32),
            shape(user_rows // 2, width, BF16),
            shape(item_rows // 2, width, F32),
        ],
        [shape(width, pairs, BF16)],
        [item_short, user_hot, grads, item_hot, item_terms],
        12,
        2.0,
    )

    def scatter(keep, send, axis, crossed):
        steps = round_steps(lax.axis_size(axis), crossed)[::-1]
        for at, step in enumerate(steps):
            got = exchange(send, axis, step)
            total = keep + got.astype(F32)
            if at + 1 < len(steps):
                half = total.shape[0] // 2
                keep, send = total[:half], total[half:].astype(BF16)
        return total

    return scatter(user_keep, user_send, "item", 0), scatter(item_keep, item_send, "user", 1)


def solution(mesh):
    split = P(("user", "item"))
    rows = P(("user", "item"), None)
    in_specs = (rows, rows, P(), P(), P(), P(), P(), split, split, split)

    return jax.shard_map(local, mesh=mesh, in_specs=in_specs, out_specs=(rows, rows), check_vma=False)
```
